32 devices in a mesh: gx: 8 (over z, x), gy: 4 (over y, core).
Axes of the slice: x: 2, y: 2, z: 4, core: 2. Of those that a mesh axis runs over, the one named last changes fastest.
Arguments:
- field: float32 [32, 384, 512], P(None, 'gx', 'gy'), may hold values from -3 to 6
- conductivity: float32 [32, 384, 512], P(None, 'gx', 'gy'), may hold values from 1 to 8
Outputs:
- updated: float32 [32, 384, 512], P(None, 'gx', 'gy')
The draws below stay inside these ranges and needn't reach their ends.
All inputs are finite; a program needn't handle non-finite values.
Results may differ from the reference program's by a relative error of at most 0.004.
Values sent between devices are 32-bit elements; how exact they have to be, the bound alone decides.
A program may use at most 512 MiB of HBM per device.

```python
import math
import jax
import jax.numpy as jnp
from jax import lax

SLAB = 32
NX = 384
NY = 512
XCOUPLE = 9216
YCOUPLE = 16384


def draw_field(key, part):
    keys = jax.random.split(jax.random.fold_in(key, 17), 3)
    rough = jnp.clip(jax.random.normal(keys[0], (SLAB, NX, NY), jnp.float32), -4.0, 4.0)
    offset = 1.5
    phases = jax.random.uniform(keys[1], (2,), jnp.float32, 0.0, 2.0 * math.pi)
    waves = jax.random.uniform(keys[2], (2,), jnp.float32, 1.0, 3.0)
    across = (jnp.arange(NX, dtype=jnp.float32) + 0.5) / NX
    along = (jnp.arange(NY, dtype=jnp.float32) + 0.5) / NY
    smooth = offset + 0.5 * jnp.sin(math.pi * waves[0] * across + phases[0])[:, None] * jnp.cos(math.pi * waves[1] * along + phases[1])[None, :]
    return rough + smooth[None]


def levels(key, dims, pieces, smallest, largest):
    loudness = 1.0
    for axis_at, blocks in pieces:
        steps = jax.random.uniform(jax.random.fold_in(jax.random.fold_in(key, 6), axis_at), (blocks,), jnp.float32, smallest / len(pieces), largest / len(pieces))
        loudness = loudness * jnp.repeat(jnp.exp(steps), dims[axis_at] // blocks).reshape((-1,) + (1,) * (len(dims) - 1 - axis_at))
    return loudness


def setup_inputs(seed: int = 0) -> dict:
    arg_keys = jax.random.split(jax.random.key(seed), 3)
    return {
        "field": draw_field(jax.random.fold_in(arg_keys[2], 71), 0),
        "conductivity": jnp.clip(jnp.exp(math.log(8.0) - 2.0794415 * jax.random.uniform(arg_keys[1], (SLAB, NX, NY), jnp.float32) ** levels(arg_keys[1], (SLAB, NX, NY), ((1, 8), (2, 4)), -0.2, 0.2)), 1.0, 8.0),
    }


depth_step = 8.0
implicit_weight = 0.5

def neighbours(values, axis):
    count = values.shape[axis]
    widths = [(0, 0)] * values.ndim
    widths[axis] = (1, 1)
    padded = jnp.pad(values, widths)
    before = lax.slice_in_dim(padded, 0, count, axis=axis)
    after = lax.slice_in_dim(padded, 2, count + 2, axis=axis)
    return (before, after)

def face_pair(conductivity, axis):
    before, after = neighbours(conductivity, axis)
    return (0.5 * (conductivity + before), 0.5 * (conductivity + after))

def flux_term(field, minus, plus, axis):
    before, after = neighbours(field, axis)
    return plus * (after - field) - minus * (field - before)

def line_solve(minus, plus, right_side, axis, coupling):
    below = jnp.moveaxis(-coupling * minus, axis, -1)
    above = jnp.moveaxis(-coupling * plus, axis, -1)
    diagonal = jnp.moveaxis(1.0 + coupling * (minus + plus), axis, -1)
    below = below.at[..., 0].set(0.0)
    above = above.at[..., -1].set(0.0)
    moved = jnp.moveaxis(right_side, axis, -1)
    solved = lax.linalg.tridiagonal_solve(below, diagonal, above, moved[..., None])[..., 0]
    return jnp.moveaxis(solved, -1, axis)

def reference(field, conductivity):
    x_couple = float(XCOUPLE)
    y_couple = float(YCOUPLE)
    minus_z, plus_z = face_pair(conductivity, 0)
    minus_x, plus_x = face_pair(conductivity, 1)
    minus_y, plus_y = face_pair(conductivity, 2)
    flux_x = flux_term(field, minus_x, plus_x, 1)
    flux_y = flux_term(field, minus_y, plus_y, 2)
    flux_z = flux_term(field, minus_z, plus_z, 0)
    explicit = 2.0 * x_couple * flux_x + 2.0 * y_couple * flux_y + depth_step * flux_z
    depth_coupling = implicit_weight * depth_step
    first_section = line_solve(minus_x, plus_x, explicit, 1, x_couple)
    second_section = line_solve(minus_y, plus_y, first_section, 2, y_couple)
    third_section = line_solve(minus_z, plus_z, second_section, 0, depth_coupling)
    return field + third_section
```

```python
import functools

import jax
import jax.numpy as jnp
from jax import lax
from jax.experimental import pallas as pl
from jax.experimental.pallas import tpu as pltpu
from jax.sharding import PartitionSpec as P

MESH = pl.DeviceIdType.MESH
F32 = jnp.float32
depth_step = 8.0
implicit_weight = 0.5

LANES = 128
SUBS = 8
PAD = SUBS
X_CHUNKS = 4


def ceil8(rows):
    return (rows + 7) // 8 * 8


def eliminate_cell(state, g):
    a, h, ground_left = state
    q = 1.0 / (a + h + g)
    w = g * q
    p = h * q
    return (a * w, h * w, ground_left + a * p), (w, p, q)


def combine_coeffs(parts):
    count = len(parts)

    def ground(k):
        return parts[k][0] + parts[k + 1][2] if k + 1 < count else parts[k][0]

    a, h, left = ground(0), parts[0][1], parts[0][2]
    kept = []
    for k in range(count - 1):
        (passed, h, left), factors = eliminate_cell((a, h, left), parts[k + 1][1])
        a = ground(k + 1) + passed
        kept.append(factors)
    return (a, h, left), kept


def combine_sources(parts, kept):
    count = len(parts)

    def source(k):
        return parts[k][0] + parts[k + 1][1] if k + 1 < count else parts[k][0]

    r, left = source(0), parts[0][1]
    scaled = []
    for k in range(count - 1):
        w, p, q = kept[k]
        left = left + r * p
        scaled.append(r * q)
        r = source(k + 1) + r * w
    return (r, left), scaled


def expand(own, before, kept, scaled):
    values = [own]
    for k in range(len(kept) - 1, -1, -1):
        w, p, _ = kept[k]
        values.append(scaled[k] + p * before + w * values[-1])
    return values[::-1]


def global_coeffs(parts):
    count = len(parts)

    def ground(d):
        return parts[d][0] + parts[d + 1][2] if d + 1 < count else parts[d][0]

    e = ground(0) + parts[0][1]
    kept = []
    for d in range(count - 1):
        g = parts[d + 1][1]
        q = 1.0 / (e + g)
        w = g * q
        kept.append((w, q))
        e = ground(d + 1) + e * w
    kept.append((None, 1.0 / e))
    return kept


def global_solve(parts, kept):
    count = len(parts)

    def source(d):
        return parts[d][0] + parts[d + 1][1] if d + 1 < count else parts[d][0]

    r = source(0)
    scaled = []
    for d in range(count - 1):
        w, q = kept[d]
        scaled.append(r * q)
        r = source(d + 1) + r * w
    values = [r * kept[-1][1]]
    for d in range(count - 2, -1, -1):
        values.append(scaled[d] + kept[d][0] * values[-1])
    return values[::-1]


def kernel(
    sizes, f_ref, c_ref, out_ref,
    tf, tc, te, ts, tv, ex, fs,
    gyc, wy, py, qy, sy, scr, vo, vp, vnodes,
    gx_, wx, px, qx, sx, wz, qz,
    xs, xr, ys, yr, xc_s, xc_r, xr_s, xr_r, xv_s, xv_r, yc_s, yc_r, yr_s, yr_r,
    ssem, rsem,
):
    nz, nx, dx, dy, x_half, y_half, z_half = sizes
    rows = nz * nx
    blocks = rows // LANES
    span = LANES + 2 * PAD
    my = LANES // SUBS
    mx = nx // X_CHUNKS
    zc = nz // dx
    ix = lax.axis_index("gx")
    iy = lax.axis_index("gy")

    barrier = pltpu.get_barrier_semaphore()
    for k in range(1, dx):
        pl.semaphore_signal(
            barrier, inc=1, device_id={"gx": lax.rem(ix + k, dx)}, device_id_type=MESH
        )
    for k in range(1, dy):
        pl.semaphore_signal(
            barrier, inc=1, device_id={"gy": lax.rem(iy + k, dy)}, device_id_type=MESH
        )

    def remote(src, dst, at, target):
        return pltpu.make_async_remote_copy(
            src_ref=src, dst_ref=dst, send_sem=ssem.at[at], recv_sem=rsem.at[at],
            device_id=target, device_id_type=MESH,
        )

    for b in range(blocks):
        tf[pl.ds(b * span + PAD, LANES), :] = f_ref[pl.ds(b * LANES, LANES), :].T
        tc[pl.ds(b * span + PAD, LANES), :] = c_ref[pl.ds(b * LANES, LANES), :].T
    for side, place in ((0, nx - 1), (1, 0)):
        xs[side, 0] = f_ref[pl.ds(place, nz, stride=nx), :]
        xs[side, 1] = c_ref[pl.ds(place, nz, stride=nx), :]
    for side, place in ((0, LANES - 1), (1, 0)):
        ys[side, 0, :blocks] = tf[pl.ds(PAD + place, blocks, stride=span), :]
        ys[side, 1, :blocks] = tc[pl.ds(PAD + place, blocks, stride=span), :]

    pl.semaphore_wait(barrier, dx + dy - 2)

    x_up = remote(xs.at[0], xr.at[0], 0, {"gx": jnp.minimum(ix + 1, dx - 1)})
    x_down = remote(xs.at[1], xr.at[1], 1, {"gx": jnp.maximum(ix - 1, 0)})
    y_up = remote(ys.at[0], yr.at[0], 2, {"gy": jnp.minimum(iy + 1, dy - 1)})
    y_down = remote(ys.at[1], yr.at[1], 3, {"gy": jnp.maximum(iy - 1, 0)})
    for inside, copy in (
        (ix < dx - 1, x_up), (ix > 0, x_down), (iy < dy - 1, y_up), (iy > 0, y_down)
    ):
        pl.when(inside)(copy.start)

    def plane(ref, z):
        return ref[pl.ds(z * nx, nx), :]

    c_here, f_here = plane(c_ref, 0), plane(f_ref, 0)
    g = z_half * c_here
    excess = 1.0 + g
    flux = g * f_here
    for z in range(nz):
        if z + 1 < nz:
            c_next, f_next = plane(c_ref, z + 1), plane(f_ref, z + 1)
            g = z_half * (c_here + c_next)
            new_flux = g * (f_next - f_here)
        else:
            c_next, f_next = None, None
            g = z_half * c_here
            new_flux = -g * f_here
        q = 1.0 / (excess + g)
        w = g * q
        qz[pl.ds(z * nx, nx), :] = q
        wz[pl.ds(z * nx, nx), :] = w
        ex[pl.ds(z * nx, nx), :] = 2.0 * (new_flux - flux)
        excess = 1.0 + excess * w
        c_here, f_here, flux = c_next, f_next, new_flux

    def x_halo(side, inside, copy):
        pl.when(inside)(copy.wait_recv)

        @pl.when(jnp.logical_not(inside))
        def _():
            xr[side] = jnp.zeros(xr.shape[1:], F32)

    x_halo(0, ix > 0, x_up)
    x_halo(1, ix < dx - 1, x_down)

    def load_x(ref, which, j):
        pieces = []
        for k in range(X_CHUNKS):
            place = k * mx + j
            if place < 0:
                pieces.append(xr[0, which])
            elif place >= nx:
                pieces.append(xr[1, which])
            else:
                pieces.append(ref[pl.ds(place, nz, stride=nx), :])
        return jnp.concatenate(pieces, axis=0)

    c_here = load_x(c_ref, 1, 0)
    g = x_half * (load_x(c_ref, 1, -1) + c_here)
    gx_[0] = g
    state = (jnp.ones_like(g), g, jnp.zeros_like(g))
    for j in range(mx):
        c_next = load_x(c_ref, 1, j + 1)
        g = x_half * (c_here + c_next)
        gx_[j + 1] = g
        if j < mx - 1:
            (passed, h, left), (w, p, q) = eliminate_cell(state, g)
            wx[j], px[j], qx[j] = w, p, q
            state = (1.0 + passed, h, left)
        c_here = c_next

    def x_parts(arrays):
        return [tuple(v[k * nz : (k + 1) * nz] for v in arrays) for k in range(X_CHUNKS)]

    (a, h, left), x_kept = combine_coeffs(x_parts(state))
    a = a + jnp.where(ix == dx - 1, 1.0, 0.0) * g[(X_CHUNKS - 1) * nz :]
    for d in range(dx):
        for at, v in enumerate((a, h, left)):
            xc_s[d, at * zc : (at + 1) * zc] = v[d * zc : (d + 1) * zc]

    sems = [4]

    def spread(axis, count, src, dst):
        me = lax.axis_index(axis)
        copies = []
        for k in range(1, count):
            peer = lax.rem(me + k, count)
            piece = src.at[peer] if axis == "gx" else src
            copies.append(remote(piece, dst.at[me], sems[0], {axis: peer}))
            copies[-1].start()
            sems[0] += 1
        dst[me] = src[me] if axis == "gx" else src[...]
        return copies

    xc_copies = spread("gx", dx, xc_s, xc_r)

    def y_halo(side, inside, copy, place):
        pl.when(inside)(copy.wait_recv)

        @pl.when(jnp.logical_not(inside))
        def _():
            yr[side] = jnp.zeros(yr.shape[1:], F32)

        tf[pl.ds(place, blocks, stride=span), :] = yr[side, 0, :blocks]
        tc[pl.ds(place, blocks, stride=span), :] = yr[side, 1, :blocks]

    y_halo(0, iy > 0, y_up, PAD - 1)
    y_halo(1, iy < dy - 1, y_down, PAD + LANES)

    def load_y(ref, j, height, offset):
        return jnp.concatenate(
            [ref[pl.ds(b * height + offset + j, SUBS, stride=my), :] for b in range(blocks)],
            axis=0,
        )

    def store_y(ref, j, values):
        for b in range(blocks):
            ref[pl.ds(b * LANES + j, SUBS, stride=my), :] = values[b * SUBS : (b + 1) * SUBS]

    c_here, f_here = load_y(tc, 0, span, PAD), load_y(tf, 0, span, PAD)
    g = y_half * (load_y(tc, -1, span, PAD) + c_here)
    gyc[0] = g
    flux = g * (f_here - load_y(tf, -1, span, PAD))
    for j in range(my):
        c_next, f_next = load_y(tc, j + 1, span, PAD), load_y(tf, j + 1, span, PAD)
        g = y_half * (c_here + c_next)
        gyc[j + 1] = g
        new_flux = g * (f_next - f_here)
        store_y(te, j, 2.0 * (new_flux - flux))
        c_here, f_here, flux = c_next, f_next, new_flux
    for b in range(blocks):
        ex[pl.ds(b * LANES, LANES), :] += te[pl.ds(b * LANES, LANES), :].T

    f_here = load_x(f_ref, 0, 0)
    flux = gx_[0] * (f_here - load_x(f_ref, 0, -1))
    r = None
    for j in range(mx):
        f_next = load_x(f_ref, 0, j + 1)
        new_flux = gx_[j + 1] * (f_next - f_here)
        source = 2.0 * (new_flux - flux) + load_x(ex, None, j)
        if r is None:
            r, left = source, jnp.zeros_like(source)
        else:
            left = left + r * px[j - 1]
            sx[j - 1] = r * qx[j - 1]
            r = source + r * wx[j - 1]
        f_here, flux = f_next, new_flux
    (r, left), x_scaled = combine_sources(x_parts((r, left)), x_kept)
    for d in range(dx):
        for at, v in enumerate((r, left)):
            xr_s[d, at * zc : (at + 1) * zc] = v[d * zc : (d + 1) * zc]
    xr_copies = spread("gx", dx, xr_s, xr_r)

    g = gyc[0]
    state = (jnp.ones_like(g), g, jnp.zeros_like(g))
    for j in range(my - 1):
        (passed, h, left), (w, p, q) = eliminate_cell(state, gyc[j + 1])
        wy[j], py[j], qy[j] = w, p, q
        state = (1.0 + passed, h, left)

    def y_parts(arrays):
        for at, v in enumerate(arrays):
            scr[at] = v
        return [
            tuple(scr[at, pl.ds(s, blocks, stride=SUBS), :] for at in range(len(arrays)))
            for s in range(SUBS)
        ]

    parts = y_parts((*state, gyc[my]))
    (a, h, left), y_kept = combine_coeffs([part[:3] for part in parts])
    a = a + jnp.where(iy == dy - 1, 1.0, 0.0) * parts[-1][3]
    for at, v in enumerate((a, h, left)):
        yc_s[at, :blocks] = v
    yc_copies = spread("gy", dy, yc_s, yc_r)

    for copy in xc_copies:
        copy.wait_recv()
    x_global = global_coeffs(
        [tuple(xc_r[d, at * zc : (at + 1) * zc] for at in range(3)) for d in range(dx)]
    )
    for copy in xr_copies:
        copy.wait_recv()
    nodes = global_solve(
        [tuple(xr_r[d, at * zc : (at + 1) * zc] for at in range(2)) for d in range(dx)], x_global
    )
    for d in range(dx):
        xv_s[d, :zc] = nodes[d - 1] if d else jnp.zeros_like(nodes[0])
        xv_s[d, zc : 2 * zc] = nodes[d]
    xv_copies = spread("gx", dx, xv_s, xv_r)
    for copy in yc_copies:
        copy.wait_recv()
    y_global = global_coeffs(
        [tuple(yc_r[d, at, :blocks] for at in range(3)) for d in range(dy)]
    )
    for copy in xv_copies:
        copy.wait_recv()
    before = jnp.concatenate([xv_r[d, :zc] for d in range(dx)], axis=0)
    own = jnp.concatenate([xv_r[d, zc : 2 * zc] for d in range(dx)], axis=0)
    ends = expand(own, before, x_kept, x_scaled)
    v = jnp.concatenate(ends, axis=0)
    before = jnp.concatenate([before] + ends[:-1], axis=0)
    for j in range(mx - 1, -1, -1):
        if j < mx - 1:
            v = sx[j] + px[j] * before + wx[j] * v
        for k in range(X_CHUNKS):
            fs[pl.ds(k * mx + j, nz, stride=nx), :] = v[k * nz : (k + 1) * nz]

    for b in range(blocks):
        ts[pl.ds(b * LANES, LANES), :] = fs[pl.ds(b * LANES, LANES), :].T
    r = load_y(ts, 0, LANES, 0)
    left = jnp.zeros_like(r)
    for j in range(my - 1):
        left = left + r * py[j]
        sy[j] = r * qy[j]
        r = load_y(ts, j + 1, LANES, 0) + r * wy[j]
    (r, left), y_scaled = combine_sources(y_parts((r, left)), y_kept)
    yr_s[0, :blocks] = r
    yr_s[1, :blocks] = left
    yr_copies = spread("gy", dy, yr_s, yr_r)
    for copy in yr_copies:
        copy.wait_recv()
    nodes = global_solve(
        [tuple(yr_r[d, at, :blocks] for at in range(2)) for d in range(dy)], y_global
    )
    vnodes[0, :blocks] = jnp.zeros_like(nodes[0])
    for d in range(dy):
        vnodes[d + 1, :blocks] = nodes[d]
    before = vnodes[iy, :blocks]
    own = vnodes[iy + 1, :blocks]
    ends = expand(own, before, y_kept, y_scaled)
    for s in range(SUBS):
        vo[pl.ds(s, blocks, stride=SUBS), :] = ends[s]
        vp[pl.ds(s, blocks, stride=SUBS), :] = ends[s - 1] if s else before
    v = vo[...]
    before = vp[...]
    for j in range(my - 1, -1, -1):
        if j < my - 1:
            v = sy[j] + py[j] * before + wy[j] * v
        store_y(tv, j, v)
    for b in range(blocks):
        fs[pl.ds(b * LANES, LANES), :] = tv[pl.ds(b * LANES, LANES), :].T

    r = plane(fs, 0)
    for z in range(nz):
        fs[pl.ds(z * nx, nx), :] = r * plane(qz, z)
        if z + 1 < nz:
            r = plane(fs, z + 1) + r * plane(wz, z)
    v = None
    for z in range(nz - 1, -1, -1):
        v = plane(fs, z) if v is None else plane(fs, z) + plane(wz, z) * v
        out_ref[pl.ds(z * nx, nx), :] = plane(f_ref, z) + v

    for sent, copy in (
        (ix < dx - 1, x_up), (ix > 0, x_down), (iy < dy - 1, y_up), (iy > 0, y_down)
    ):
        pl.when(sent)(copy.wait_send)
    for copies in (xc_copies, xr_copies, xv_copies, yc_copies, yr_copies):
        for copy in copies:
            copy.wait_send()


def on_device(dx, dy, field, conductivity):
    nz, nx, ny = field.shape
    rows = nz * nx
    blocks = rows // LANES
    total_x = nx * dx
    total_y = ny * dy
    x_half = 0.5 * float(total_x * total_x // 16)
    y_half = 0.5 * float(total_y * total_y // 16)
    z_half = 0.5 * implicit_weight * depth_step
    zc = nz // dx
    span = LANES + 2 * PAD
    my = LANES // SUBS
    mx = nx // X_CHUNKS
    xrows = X_CHUNKS * nz
    yrows = blocks * SUBS
    b16 = ceil8(blocks)
    nsem = 4 + 3 * (dx - 1) + 2 * (dy - 1)

    def vmem(*shape):
        return pltpu.VMEM(shape, F32)

    grid = vmem(rows, LANES)
    out = pl.pallas_call(
        functools.partial(kernel, (nz, nx, dx, dy, x_half, y_half, z_half)),
        out_shape=jax.ShapeDtypeStruct((rows, LANES), F32),
        in_specs=[pl.BlockSpec(memory_space=pltpu.VMEM)] * 2,
        out_specs=pl.BlockSpec(memory_space=pltpu.VMEM),
        scratch_shapes=[
            vmem(blocks * span, LANES), vmem(blocks * span, LANES), grid, grid, grid, grid, grid,
            vmem(my + 1, yrows, LANES),
            vmem(my - 1, yrows, LANES), vmem(my - 1, yrows, LANES), vmem(my - 1, yrows, LANES),
            vmem(my - 1, yrows, LANES),
            vmem(4, yrows, LANES), vmem(yrows, LANES), vmem(yrows, LANES),
            vmem(dy + 1, b16, LANES),
            vmem(mx + 1, xrows, LANES),
            vmem(mx - 1, xrows, LANES), vmem(mx - 1, xrows, LANES), vmem(mx - 1, xrows, LANES),
            vmem(mx - 1, xrows, LANES),
            grid, grid,
            vmem(2, 2, nz, LANES), vmem(2, 2, nz, LANES),
            vmem(2, 2, b16, LANES), vmem(2, 2, b16, LANES),
            vmem(dx, ceil8(3 * zc), LANES), vmem(dx, ceil8(3 * zc), LANES),
            vmem(dx, ceil8(2 * zc), LANES), vmem(dx, ceil8(2 * zc), LANES),
            vmem(dx, ceil8(2 * zc), LANES), vmem(dx, ceil8(2 * zc), LANES),
            vmem(3, b16, LANES), vmem(dy, 3, b16, LANES),
            vmem(2, b16, LANES), vmem(dy, 2, b16, LANES),
            pltpu.SemaphoreType.DMA((nsem,)), pltpu.SemaphoreType.DMA((nsem,)),
        ],
        compiler_params=pltpu.CompilerParams(
            collective_id=0, has_side_effects=True, vmem_limit_bytes=48 << 20
        ),
    )(field.reshape(rows, ny), conductivity.reshape(rows, ny))
    return out.reshape(nz, nx, ny)


def solution(mesh):
    return jax.shard_map(
        functools.partial(on_device, mesh.shape["gx"], mesh.shape["gy"]),
        mesh=mesh,
        in_specs=(P(None, "gx", "gy"), P(None, "gx", "gy")),
        out_specs=P(None, "gx", "gy"),
        check_vma=False,
    )
```

```python
import functools

import jax
import jax.numpy as jnp
from jax import lax
from jax.experimental import pallas as pl
from jax.experimental.pallas import tpu as pltpu
from jax.sharding import PartitionSpec as P

MESH = pl.DeviceIdType.MESH
F32 = jnp.float32
depth_step = 8.0
implicit_weight = 0.5

LANES = 128
SUBS = 8
PAD = SUBS
X_CHUNKS = 4
LOADS = 4
STORES = 4


def ceil8(rows):
    return (rows + 7) // 8 * 8


def eliminate_cell(state, g):
    a, h, ground_left = state
    q = 1.0 / (a + h + g)
    w = g * q
    p = h * q
    return (a * w, h * w, ground_left + a * p), (w, p, q)


def combine_coeffs(parts):
    count = len(parts)

    def ground(k):
        return parts[k][0] + parts[k + 1][2] if k + 1 < count else parts[k][0]

    a, h, left = ground(0), parts[0][1], parts[0][2]
    kept = []
    for k in range(count - 1):
        (passed, h, left), factors = eliminate_cell((a, h, left), parts[k + 1][1])
        a = ground(k + 1) + passed
        kept.append(factors)
    return (a, h, left), kept


def combine_sources(parts, kept):
    count = len(parts)

    def source(k):
        return parts[k][0] + parts[k + 1][1] if k + 1 < count else parts[k][0]

    r, left = source(0), parts[0][1]
    scaled = []
    for k in range(count - 1):
        w, p, q = kept[k]
        left = left + r * p
        scaled.append(r * q)
        r = source(k + 1) + r * w
    return (r, left), scaled


def expand(own, before, kept, scaled):
    values = [own]
    for k in range(len(kept) - 1, -1, -1):
        w, p, _ = kept[k]
        values.append(scaled[k] + p * before + w * values[-1])
    return values[::-1]


def global_coeffs(parts):
    count = len(parts)

    def ground(d):
        return parts[d][0] + parts[d + 1][2] if d + 1 < count else parts[d][0]

    e = ground(0) + parts[0][1]
    kept = []
    for d in range(count - 1):
        g = parts[d + 1][1]
        q = 1.0 / (e + g)
        w = g * q
        kept.append((w, q))
        e = ground(d + 1) + e * w
    kept.append((None, 1.0 / e))
    return kept


def global_solve(parts, kept):
    count = len(parts)

    def source(d):
        return parts[d][0] + parts[d + 1][1] if d + 1 < count else parts[d][0]

    r = source(0)
    scaled = []
    for d in range(count - 1):
        w, q = kept[d]
        scaled.append(r * q)
        r = source(d + 1) + r * w
    values = [r * kept[-1][1]]
    for d in range(count - 2, -1, -1):
        values.append(scaled[d] + kept[d][0] * values[-1])
    return values[::-1]


def kernel(
    sizes, f_hbm, c_hbm, out_hbm,
    f_ref, c_ref, out_ref,
    tf, tc, te, ts, tv, ex, fs,
    gyc, wy, py, qy, sy, scr, vo, vp, vnodes,
    gx_, wx, px, qx, sx, wz, qz,
    xs, xr, ys, yr, xc_s, xc_r, xr_s, xr_r, xv_s, xv_r, yc_s, yc_r, yr_s, yr_r,
    ssem, rsem, lsem,
):
    nz, nx, dx, dy, x_half, y_half, z_half = sizes
    rows = nz * nx
    blocks = rows // LANES
    span = LANES + 2 * PAD
    my = LANES // SUBS
    mx = nx // X_CHUNKS
    zc = nz // dx
    ix = lax.axis_index("gx")
    iy = lax.axis_index("gy")

    barrier = pltpu.get_barrier_semaphore()
    for k in range(1, dx):
        pl.semaphore_signal(
            barrier, inc=1, device_id={"gx": lax.rem(ix + k, dx)}, device_id_type=MESH
        )
    for k in range(1, dy):
        pl.semaphore_signal(
            barrier, inc=1, device_id={"gy": lax.rem(iy + k, dy)}, device_id_type=MESH
        )

    loads = []
    piece = blocks // LOADS * LANES
    for k in range(LOADS):
        for at, (src, dst) in enumerate(((c_hbm, c_ref), (f_hbm, f_ref))):
            part = pl.ds(k * piece, piece)
            loads.append(pltpu.make_async_copy(src.at[part], dst.at[part], lsem.at[2 * k + at]))
            loads[-1].start()

    def remote(src, dst, at, target):
        return pltpu.make_async_remote_copy(
            src_ref=src, dst_ref=dst, send_sem=ssem.at[at], recv_sem=rsem.at[at],
            device_id=target, device_id_type=MESH,
        )

    for b in range(blocks):
        if b % (blocks // LOADS) == 0:
            at = 2 * (b // (blocks // LOADS))
            loads[at].wait()
            loads[at + 1].wait()
        tf[pl.ds(b * span + PAD, LANES), :] = f_ref[pl.ds(b * LANES, LANES), :].T
        tc[pl.ds(b * span + PAD, LANES), :] = c_ref[pl.ds(b * LANES, LANES), :].T
    for side, place in ((0, nx - 1), (1, 0)):
        xs[side, 0] = f_ref[pl.ds(place, nz, stride=nx), :]
        xs[side, 1] = c_ref[pl.ds(place, nz, stride=nx), :]
    for side, place in ((0, LANES - 1), (1, 0)):
        ys[side, 0, :blocks] = tf[pl.ds(PAD + place, blocks, stride=span), :]
        ys[side, 1, :blocks] = tc[pl.ds(PAD + place, blocks, stride=span), :]

    def plane(ref, z):
        return ref[pl.ds(z * nx, nx), :]

    c_here, f_here = plane(c_ref, 0), plane(f_ref, 0)
    g = z_half * c_here
    excess = 1.0 + g
    flux = g * f_here
    for z in range(nz):
        if z + 1 < nz:
            c_next, f_next = plane(c_ref, z + 1), plane(f_ref, z + 1)
            g = z_half * (c_here + c_next)
            new_flux = g * (f_next - f_here)
        else:
            c_next, f_next = None, None
            g = z_half * c_here
            new_flux = -g * f_here
        q = 1.0 / (excess + g)
        w = g * q
        qz[pl.ds(z * nx, nx), :] = q
        wz[pl.ds(z * nx, nx), :] = w
        ex[pl.ds(z * nx, nx), :] = 2.0 * (new_flux - flux)
        excess = 1.0 + excess * w
        c_here, f_here, flux = c_next, f_next, new_flux

    pl.semaphore_wait(barrier, dx + dy - 2)

    x_up = remote(xs.at[0], xr.at[0], 0, {"gx": jnp.minimum(ix + 1, dx - 1)})
    x_down = remote(xs.at[1], xr.at[1], 1, {"gx": jnp.maximum(ix - 1, 0)})
    y_up = remote(ys.at[0], yr.at[0], 2, {"gy": jnp.minimum(iy + 1, dy - 1)})
    y_down = remote(ys.at[1], yr.at[1], 3, {"gy": jnp.maximum(iy - 1, 0)})
    for inside, copy in (
        (ix < dx - 1, x_up), (ix > 0, x_down), (iy < dy - 1, y_up), (iy > 0, y_down)
    ):
        pl.when(inside)(copy.start)

    def x_halo(side, inside, copy):
        pl.when(inside)(copy.wait_recv)

        @pl.when(jnp.logical_not(inside))
        def _():
            xr[side] = jnp.zeros(xr.shape[1:], F32)

    x_halo(0, ix > 0, x_up)
    x_halo(1, ix < dx - 1, x_down)

    def load_x(ref, which, j):
        pieces = []
        for k in range(X_CHUNKS):
            place = k * mx + j
            if place < 0:
                pieces.append(xr[0, which])
            elif place >= nx:
                pieces.append(xr[1, which])
            else:
                pieces.append(ref[pl.ds(place, nz, stride=nx), :])
        return jnp.concatenate(pieces, axis=0)

    c_here = load_x(c_ref, 1, 0)
    g = x_half * (load_x(c_ref, 1, -1) + c_here)
    gx_[0] = g
    state = (jnp.ones_like(g), g, jnp.zeros_like(g))
    for j in range(mx):
        c_next = load_x(c_ref, 1, j + 1)
        g = x_half * (c_here + c_next)
        gx_[j + 1] = g
        if j < mx - 1:
            (passed, h, left), (w, p, q) = eliminate_cell(state, g)
            wx[j], px[j], qx[j] = w, p, q
            state = (1.0 + passed, h, left)
        c_here = c_next

    def x_parts(arrays):
        return [tuple(v[k * nz : (k + 1) * nz] for v in arrays) for k in range(X_CHUNKS)]

    (a, h, left), x_kept = combine_coeffs(x_parts(state))
    a = a + jnp.where(ix == dx - 1, 1.0, 0.0) * g[(X_CHUNKS - 1) * nz :]
    for d in range(dx):
        for at, v in enumerate((a, h, left)):
            xc_s[d, at * zc : (at + 1) * zc] = v[d * zc : (d + 1) * zc]

    sems = [4]

    def spread(axis, count, src, dst):
        me = lax.axis_index(axis)
        copies = []
        for k in range(1, count):
            peer = lax.rem(me + k, count)
            piece = src.at[peer] if axis == "gx" else src
            copies.append(remote(piece, dst.at[me], sems[0], {axis: peer}))
            copies[-1].start()
            sems[0] += 1
        dst[me] = src[me] if axis == "gx" else src[...]
        return copies

    xc_copies = spread("gx", dx, xc_s, xc_r)

    def y_halo(side, inside, copy, place):
        pl.when(inside)(copy.wait_recv)

        @pl.when(jnp.logical_not(inside))
        def _():
            yr[side] = jnp.zeros(yr.shape[1:], F32)

        tf[pl.ds(place, blocks, stride=span), :] = yr[side, 0, :blocks]
        tc[pl.ds(place, blocks, stride=span), :] = yr[side, 1, :blocks]

    y_halo(0, iy > 0, y_up, PAD - 1)
    y_halo(1, iy < dy - 1, y_down, PAD + LANES)

    def load_y(ref, j, height, offset):
        return jnp.concatenate(
            [ref[pl.ds(b * height + offset + j, SUBS, stride=my), :] for b in range(blocks)],
            axis=0,
        )

    def store_y(ref, j, values):
        for b in range(blocks):
            ref[pl.ds(b * LANES + j, SUBS, stride=my), :] = values[b * SUBS : (b + 1) * SUBS]

    c_here, f_here = load_y(tc, 0, span, PAD), load_y(tf, 0, span, PAD)
    g = y_half * (load_y(tc, -1, span, PAD) + c_here)
    gyc[0] = g
    flux = g * (f_here - load_y(tf, -1, span, PAD))
    for j in range(my):
        c_next, f_next = load_y(tc, j + 1, span, PAD), load_y(tf, j + 1, span, PAD)
        g = y_half * (c_here + c_next)
        gyc[j + 1] = g
        new_flux = g * (f_next - f_here)
        store_y(te, j, 2.0 * (new_flux - flux))
        c_here, f_here, flux = c_next, f_next, new_flux
    for b in range(blocks):
        ex[pl.ds(b * LANES, LANES), :] += te[pl.ds(b * LANES, LANES), :].T

    f_here = load_x(f_ref, 0, 0)
    flux = gx_[0] * (f_here - load_x(f_ref, 0, -1))
    r = None
    for j in range(mx):
        f_next = load_x(f_ref, 0, j + 1)
        new_flux = gx_[j + 1] * (f_next - f_here)
        source = 2.0 * (new_flux - flux) + load_x(ex, None, j)
        if r is None:
            r, left = source, jnp.zeros_like(source)
        else:
            left = left + r * px[j - 1]
            sx[j - 1] = r * qx[j - 1]
            r = source + r * wx[j - 1]
        f_here, flux = f_next, new_flux
    (r, left), x_scaled = combine_sources(x_parts((r, left)), x_kept)
    for d in range(dx):
        for at, v in enumerate((r, left)):
            xr_s[d, at * zc : (at + 1) * zc] = v[d * zc : (d + 1) * zc]
    xr_copies = spread("gx", dx, xr_s, xr_r)

    g = gyc[0]
    state = (jnp.ones_like(g), g, jnp.zeros_like(g))
    for j in range(my - 1):
        (passed, h, left), (w, p, q) = eliminate_cell(state, gyc[j + 1])
        wy[j], py[j], qy[j] = w, p, q
        state = (1.0 + passed, h, left)

    def y_parts(arrays):
        for at, v in enumerate(arrays):
            scr[at] = v
        return [
            tuple(scr[at, pl.ds(s, blocks, stride=SUBS), :] for at in range(len(arrays)))
            for s in range(SUBS)
        ]

    parts = y_parts((*state, gyc[my]))
    (a, h, left), y_kept = combine_coeffs([part[:3] for part in parts])
    a = a + jnp.where(iy == dy - 1, 1.0, 0.0) * parts[-1][3]
    for at, v in enumerate((a, h, left)):
        yc_s[at, :blocks] = v
    yc_copies = spread("gy", dy, yc_s, yc_r)

    for copy in xc_copies:
        copy.wait_recv()
    x_global = global_coeffs(
        [tuple(xc_r[d, at * zc : (at + 1) * zc] for at in range(3)) for d in range(dx)]
    )
    for copy in xr_copies:
        copy.wait_recv()
    nodes = global_solve(
        [tuple(xr_r[d, at * zc : (at + 1) * zc] for at in range(2)) for d in range(dx)], x_global
    )
    for d in range(dx):
        xv_s[d, :zc] = nodes[d - 1] if d else jnp.zeros_like(nodes[0])
        xv_s[d, zc : 2 * zc] = nodes[d]
    xv_copies = spread("gx", dx, xv_s, xv_r)
    for copy in yc_copies:
        copy.wait_recv()
    y_global = global_coeffs(
        [tuple(yc_r[d, at, :blocks] for at in range(3)) for d in range(dy)]
    )
    for copy in xv_copies:
        copy.wait_recv()
    before = jnp.concatenate([xv_r[d, :zc] for d in range(dx)], axis=0)
    own = jnp.concatenate([xv_r[d, zc : 2 * zc] for d in range(dx)], axis=0)
    ends = expand(own, before, x_kept, x_scaled)
    v = jnp.concatenate(ends, axis=0)
    before = jnp.concatenate([before] + ends[:-1], axis=0)
    for j in range(mx - 1, -1, -1):
        if j < mx - 1:
            v = sx[j] + px[j] * before + wx[j] * v
        for k in range(X_CHUNKS):
            fs[pl.ds(k * mx + j, nz, stride=nx), :] = v[k * nz : (k + 1) * nz]

    for b in range(blocks):
        ts[pl.ds(b * LANES, LANES), :] = fs[pl.ds(b * LANES, LANES), :].T
    r = load_y(ts, 0, LANES, 0)
    left = jnp.zeros_like(r)
    for j in range(my - 1):
        left = left + r * py[j]
        sy[j] = r * qy[j]
        r = load_y(ts, j + 1, LANES, 0) + r * wy[j]
    (r, left), y_scaled = combine_sources(y_parts((r, left)), y_kept)
    yr_s[0, :blocks] = r
    yr_s[1, :blocks] = left
    yr_copies = spread("gy", dy, yr_s, yr_r)
    for copy in yr_copies:
        copy.wait_recv()
    nodes = global_solve(
        [tuple(yr_r[d, at, :blocks] for at in range(2)) for d in range(dy)], y_global
    )
    vnodes[0, :blocks] = jnp.zeros_like(nodes[0])
    for d in range(dy):
        vnodes[d + 1, :blocks] = nodes[d]
    before = vnodes[iy, :blocks]
    own = vnodes[iy + 1, :blocks]
    ends = expand(own, before, y_kept, y_scaled)
    for s in range(SUBS):
        vo[pl.ds(s, blocks, stride=SUBS), :] = ends[s]
        vp[pl.ds(s, blocks, stride=SUBS), :] = ends[s - 1] if s else before
    v = vo[...]
    before = vp[...]
    for j in range(my - 1, -1, -1):
        if j < my - 1:
            v = sy[j] + py[j] * before + wy[j] * v
        store_y(tv, j, v)
    for b in range(blocks):
        fs[pl.ds(b * LANES, LANES), :] = tv[pl.ds(b * LANES, LANES), :].T

    r = plane(fs, 0)
    for z in range(nz):
        fs[pl.ds(z * nx, nx), :] = r * plane(qz, z)
        if z + 1 < nz:
            r = plane(fs, z + 1) + r * plane(wz, z)
    v = None
    stores = []
    for z in range(nz - 1, -1, -1):
        v = plane(fs, z) if v is None else plane(fs, z) + plane(wz, z) * v
        out_ref[pl.ds(z * nx, nx), :] = plane(f_ref, z) + v
        if z % (nz // STORES) == 0:
            part = pl.ds(z * nx, nz // STORES * nx)
            at = 2 * LOADS + z // (nz // STORES)
            stores.append(pltpu.make_async_copy(out_ref.at[part], out_hbm.at[part], lsem.at[at]))
            stores[-1].start()

    for sent, copy in (
        (ix < dx - 1, x_up), (ix > 0, x_down), (iy < dy - 1, y_up), (iy > 0, y_down)
    ):
        pl.when(sent)(copy.wait_send)
    for copies in (xc_copies, xr_copies, xv_copies, yc_copies, yr_copies):
        for copy in copies:
            copy.wait_send()
    for copy in stores:
        copy.wait()


def on_device(dx, dy, field, conductivity):
    nz, nx, ny = field.shape
    rows = nz * nx
    blocks = rows // LANES
    total_x = nx * dx
    total_y = ny * dy
    x_half = 0.5 * float(total_x * total_x // 16)
    y_half = 0.5 * float(total_y * total_y // 16)
    z_half = 0.5 * implicit_weight * depth_step
    zc = nz // dx
    span = LANES + 2 * PAD
    my = LANES // SUBS
    mx = nx // X_CHUNKS
    xrows = X_CHUNKS * nz
    yrows = blocks * SUBS
    b16 = ceil8(blocks)
    nsem = 4 + 3 * (dx - 1) + 2 * (dy - 1)

    def vmem(*shape):
        return pltpu.VMEM(shape, F32)

    grid = vmem(rows, LANES)
    out = pl.pallas_call(
        functools.partial(kernel, (nz, nx, dx, dy, x_half, y_half, z_half)),
        out_shape=jax.ShapeDtypeStruct((rows, LANES), F32),
        in_specs=[pl.BlockSpec(memory_space=pl.ANY)] * 2,
        out_specs=pl.BlockSpec(memory_space=pl.ANY),
        scratch_shapes=[
            grid, grid, grid,
            vmem(blocks * span, LANES), vmem(blocks * span, LANES), grid, grid, grid, grid, grid,
            vmem(my + 1, yrows, LANES),
            vmem(my - 1, yrows, LANES), vmem(my - 1, yrows, LANES), vmem(my - 1, yrows, LANES),
            vmem(my - 1, yrows, LANES),
            vmem(4, yrows, LANES), vmem(yrows, LANES), vmem(yrows, LANES),
            vmem(dy + 1, b16, LANES),
            vmem(mx + 1, xrows, LANES),
            vmem(mx - 1, xrows, LANES), vmem(mx - 1, xrows, LANES), vmem(mx - 1, xrows, LANES),
            vmem(mx - 1, xrows, LANES),
            grid, grid,
            vmem(2, 2, nz, LANES), vmem(2, 2, nz, LANES),
            vmem(2, 2, b16, LANES), vmem(2, 2, b16, LANES),
            vmem(dx, ceil8(3 * zc), LANES), vmem(dx, ceil8(3 * zc), LANES),
            vmem(dx, ceil8(2 * zc), LANES), vmem(dx, ceil8(2 * zc), LANES),
            vmem(dx, ceil8(2 * zc), LANES), vmem(dx, ceil8(2 * zc), LANES),
            vmem(3, b16, LANES), vmem(dy, 3, b16, LANES),
            vmem(2, b16, LANES), vmem(dy, 2, b16, LANES),
            pltpu.SemaphoreType.DMA((nsem,)), pltpu.SemaphoreType.DMA((nsem,)),
            pltpu.SemaphoreType.DMA((2 * LOADS + STORES,)),
        ],
        compiler_params=pltpu.CompilerParams(
            collective_id=0, has_side_effects=True, vmem_limit_bytes=58 << 20
        ),
    )(field.reshape(rows, ny), conductivity.reshape(rows, ny))
    return out.reshape(nz, nx, ny)


def solution(mesh):
    return jax.shard_map(
        functools.partial(on_device, mesh.shape["gx"], mesh.shape["gy"]),
        mesh=mesh,
        in_specs=(P(None, "gx", "gy"), P(None, "gx", "gy")),
        out_specs=P(None, "gx", "gy"),
        check_vma=False,
    )
```

```python
import functools

import jax
import jax.numpy as jnp
from jax import lax
from jax.experimental import pallas as pl
from jax.experimental.pallas import tpu as pltpu
from jax.sharding import PartitionSpec as P

MESH = pl.DeviceIdType.MESH
F32 = jnp.float32
depth_step = 8.0
implicit_weight = 0.5

LANES = 128
SUBS = 8
PAD = SUBS
X_CHUNKS = 4
LOADS = 4


def ceil8(rows):
    return (rows + 7) // 8 * 8


def eliminate_cell(state, g):
    a, h, ground_left = state
    q = 1.0 / (a + h + g)
    w = g * q
    p = h * q
    return (a * w, h * w, ground_left + a * p), (w, p, q)


def combine_coeffs(parts):
    count = len(parts)

    def ground(k):
        return parts[k][0] + parts[k + 1][2] if k + 1 < count else parts[k][0]

    a, h, left = ground(0), parts[0][1], parts[0][2]
    kept = []
    for k in range(count - 1):
        (passed, h, left), factors = eliminate_cell((a, h, left), parts[k + 1][1])
        a = ground(k + 1) + passed
        kept.append(factors)
    return (a, h, left), kept


def combine_sources(parts, kept):
    count = len(parts)

    def source(k):
        return parts[k][0] + parts[k + 1][1] if k + 1 < count else parts[k][0]

    r, left = source(0), parts[0][1]
    scaled = []
    for k in range(count - 1):
        w, p, q = kept[k]
        left = left + r * p
        scaled.append(r * q)
        r = source(k + 1) + r * w
    return (r, left), scaled


def expand(own, before, kept, scaled):
    values = [own]
    for k in range(len(kept) - 1, -1, -1):
        w, p, _ = kept[k]
        values.append(scaled[k] + p * before + w * values[-1])
    return values[::-1]


def global_coeffs(parts):
    count = len(parts)

    def ground(d):
        return parts[d][0] + parts[d + 1][2] if d + 1 < count else parts[d][0]

    e = ground(0) + parts[0][1]
    kept = []
    for d in range(count - 1):
        g = parts[d + 1][1]
        q = 1.0 / (e + g)
        w = g * q
        kept.append((w, q))
        e = ground(d + 1) + e * w
    kept.append((None, 1.0 / e))
    return kept


def global_solve(parts, kept):
    count = len(parts)

    def source(d):
        return parts[d][0] + parts[d + 1][1] if d + 1 < count else parts[d][0]

    r = source(0)
    scaled = []
    for d in range(count - 1):
        w, q = kept[d]
        scaled.append(r * q)
        r = source(d + 1) + r * w
    values = [r * kept[-1][1]]
    for d in range(count - 2, -1, -1):
        values.append(scaled[d] + kept[d][0] * values[-1])
    return values[::-1]


def kernel(
    sizes, f_hbm, c_hbm, out_ref,
    f_ref, c_ref,
    tf, tc, te, ts, tv, ex, fs,
    gyc, wy, py, qy, sy, scr, vo, vp, vnodes,
    gx_, wx, px, qx, sx, wz, qz,
    xs, xr, ys, yr, xc_s, xc_r, xr_s, xr_r, xv_s, xv_r, yc_s, yc_r, yr_s, yr_r,
    ssem, rsem, lsem,
):
    nz, nx, dx, dy, x_half, y_half, z_half = sizes
    rows = nz * nx
    blocks = rows // LANES
    span = LANES + 2 * PAD
    my = LANES // SUBS
    mx = nx // X_CHUNKS
    zc = nz // dx
    ix = lax.axis_index("gx")
    iy = lax.axis_index("gy")

    barrier = pltpu.get_barrier_semaphore()
    for k in range(1, dx):
        pl.semaphore_signal(
            barrier, inc=1, device_id={"gx": lax.rem(ix + k, dx)}, device_id_type=MESH
        )
    for k in range(1, dy):
        pl.semaphore_signal(
            barrier, inc=1, device_id={"gy": lax.rem(iy + k, dy)}, device_id_type=MESH
        )

    loads = []
    piece = blocks // LOADS * LANES
    for k in range(LOADS):
        for at, (src, dst) in enumerate(((c_hbm, c_ref), (f_hbm, f_ref))):
            part = pl.ds(k * piece, piece)
            loads.append(pltpu.make_async_copy(src.at[part], dst.at[part], lsem.at[2 * k + at]))
            loads[-1].start()

    def remote(src, dst, at, target):
        return pltpu.make_async_remote_copy(
            src_ref=src, dst_ref=dst, send_sem=ssem.at[at], recv_sem=rsem.at[at],
            device_id=target, device_id_type=MESH,
        )

    for b in range(blocks):
        if b % (blocks // LOADS) == 0:
            at = 2 * (b // (blocks // LOADS))
            loads[at].wait()
            loads[at + 1].wait()
        tf[pl.ds(b * span + PAD, LANES), :] = f_ref[pl.ds(b * LANES, LANES), :].T
        tc[pl.ds(b * span + PAD, LANES), :] = c_ref[pl.ds(b * LANES, LANES), :].T
    for side, place in ((0, nx - 1), (1, 0)):
        xs[side, 0] = f_ref[pl.ds(place, nz, stride=nx), :]
        xs[side, 1] = c_ref[pl.ds(place, nz, stride=nx), :]
    for side, place in ((0, LANES - 1), (1, 0)):
        ys[side, 0, :blocks] = tf[pl.ds(PAD + place, blocks, stride=span), :]
        ys[side, 1, :blocks] = tc[pl.ds(PAD + place, blocks, stride=span), :]

    def plane(ref, z):
        return ref[pl.ds(z * nx, nx), :]

    c_here, f_here = plane(c_ref, 0), plane(f_ref, 0)
    g = z_half * c_here
    excess = 1.0 + g
    flux = g * f_here
    for z in range(nz):
        if z + 1 < nz:
            c_next, f_next = plane(c_ref, z + 1), plane(f_ref, z + 1)
            g = z_half * (c_here + c_next)
            new_flux = g * (f_next - f_here)
        else:
            c_next, f_next = None, None
            g = z_half * c_here
            new_flux = -g * f_here
        q = 1.0 / (excess + g)
        w = g * q
        qz[pl.ds(z * nx, nx), :] = q
        wz[pl.ds(z * nx, nx), :] = w
        ex[pl.ds(z * nx, nx), :] = 2.0 * (new_flux - flux)
        excess = 1.0 + excess * w
        c_here, f_here, flux = c_next, f_next, new_flux

    pl.semaphore_wait(barrier, dx + dy - 2)

    x_up = remote(xs.at[0], xr.at[0], 0, {"gx": jnp.minimum(ix + 1, dx - 1)})
    x_down = remote(xs.at[1], xr.at[1], 1, {"gx": jnp.maximum(ix - 1, 0)})
    y_up = remote(ys.at[0], yr.at[0], 2, {"gy": jnp.minimum(iy + 1, dy - 1)})
    y_down = remote(ys.at[1], yr.at[1], 3, {"gy": jnp.maximum(iy - 1, 0)})
    for inside, copy in (
        (ix < dx - 1, x_up), (ix > 0, x_down), (iy < dy - 1, y_up), (iy > 0, y_down)
    ):
        pl.when(inside)(copy.start)

    def x_halo(side, inside, copy):
        pl.when(inside)(copy.wait_recv)

        @pl.when(jnp.logical_not(inside))
        def _():
            xr[side] = jnp.zeros(xr.shape[1:], F32)

    x_halo(0, ix > 0, x_up)
    x_halo(1, ix < dx - 1, x_down)

    def load_x(ref, which, j):
        pieces = []
        for k in range(X_CHUNKS):
            place = k * mx + j
            if place < 0:
                pieces.append(xr[0, which])
            elif place >= nx:
                pieces.append(xr[1, which])
            else:
                pieces.append(ref[pl.ds(place, nz, stride=nx), :])
        return jnp.concatenate(pieces, axis=0)

    c_here = load_x(c_ref, 1, 0)
    g = x_half * (load_x(c_ref, 1, -1) + c_here)
    gx_[0] = g
    state = (jnp.ones_like(g), g, jnp.zeros_like(g))
    for j in range(mx):
        c_next = load_x(c_ref, 1, j + 1)
        g = x_half * (c_here + c_next)
        gx_[j + 1] = g
        if j < mx - 1:
            (passed, h, left), (w, p, q) = eliminate_cell(state, g)
            wx[j], px[j], qx[j] = w, p, q
            state = (1.0 + passed, h, left)
        c_here = c_next

    def x_parts(arrays):
        return [tuple(v[k * nz : (k + 1) * nz] for v in arrays) for k in range(X_CHUNKS)]

    (a, h, left), x_kept = combine_coeffs(x_parts(state))
    a = a + jnp.where(ix == dx - 1, 1.0, 0.0) * g[(X_CHUNKS - 1) * nz :]
    for d in range(dx):
        for at, v in enumerate((a, h, left)):
            xc_s[d, at * zc : (at + 1) * zc] = v[d * zc : (d + 1) * zc]

    sems = [4]

    def spread(axis, count, src, dst):
        me = lax.axis_index(axis)
        copies = []
        for k in range(1, count):
            peer = lax.rem(me + k, count)
            piece = src.at[peer] if axis == "gx" else src
            copies.append(remote(piece, dst.at[me], sems[0], {axis: peer}))
            copies[-1].start()
            sems[0] += 1
        dst[me] = src[me] if axis == "gx" else src[...]
        return copies

    xc_copies = spread("gx", dx, xc_s, xc_r)

    def y_halo(side, inside, copy, place):
        pl.when(inside)(copy.wait_recv)

        @pl.when(jnp.logical_not(inside))
        def _():
            yr[side] = jnp.zeros(yr.shape[1:], F32)

        tf[pl.ds(place, blocks, stride=span), :] = yr[side, 0, :blocks]
        tc[pl.ds(place, blocks, stride=span), :] = yr[side, 1, :blocks]

    y_halo(0, iy > 0, y_up, PAD - 1)
    y_halo(1, iy < dy - 1, y_down, PAD + LANES)

    def load_y(ref, j, height, offset):
        return jnp.concatenate(
            [ref[pl.ds(b * height + offset + j, SUBS, stride=my), :] for b in range(blocks)],
            axis=0,
        )

    def store_y(ref, j, values):
        for b in range(blocks):
            ref[pl.ds(b * LANES + j, SUBS, stride=my), :] = values[b * SUBS : (b + 1) * SUBS]

    c_here, f_here = load_y(tc, 0, span, PAD), load_y(tf, 0, span, PAD)
    g = y_half * (load_y(tc, -1, span, PAD) + c_here)
    gyc[0] = g
    flux = g * (f_here - load_y(tf, -1, span, PAD))
    for j in range(my):
        c_next, f_next = load_y(tc, j + 1, span, PAD), load_y(tf, j + 1, span, PAD)
        g = y_half * (c_here + c_next)
        gyc[j + 1] = g
        new_flux = g * (f_next - f_here)
        store_y(te, j, 2.0 * (new_flux - flux))
        c_here, f_here, flux = c_next, f_next, new_flux
    for b in range(blocks):
        ex[pl.ds(b * LANES, LANES), :] += te[pl.ds(b * LANES, LANES), :].T

    f_here = load_x(f_ref, 0, 0)
    flux = gx_[0] * (f_here - load_x(f_ref, 0, -1))
    r = None
    for j in range(mx):
        f_next = load_x(f_ref, 0, j + 1)
        new_flux = gx_[j + 1] * (f_next - f_here)
        source = 2.0 * (new_flux - flux) + load_x(ex, None, j)
        if r is None:
            r, left = source, jnp.zeros_like(source)
        else:
            left = left + r * px[j - 1]
            sx[j - 1] = r * qx[j - 1]
            r = source + r * wx[j - 1]
        f_here, flux = f_next, new_flux
    (r, left), x_scaled = combine_sources(x_parts((r, left)), x_kept)
    for d in range(dx):
        for at, v in enumerate((r, left)):
            xr_s[d, at * zc : (at + 1) * zc] = v[d * zc : (d + 1) * zc]
    xr_copies = spread("gx", dx, xr_s, xr_r)

    g = gyc[0]
    state = (jnp.ones_like(g), g, jnp.zeros_like(g))
    for j in range(my - 1):
        (passed, h, left), (w, p, q) = eliminate_cell(state, gyc[j + 1])
        wy[j], py[j], qy[j] = w, p, q
        state = (1.0 + passed, h, left)

    def y_parts(arrays):
        for at, v in enumerate(arrays):
            scr[at] = v
        return [
            tuple(scr[at, pl.ds(s, blocks, stride=SUBS), :] for at in range(len(arrays)))
            for s in range(SUBS)
        ]

    parts = y_parts((*state, gyc[my]))
    (a, h, left), y_kept = combine_coeffs([part[:3] for part in parts])
    a = a + jnp.where(iy == dy - 1, 1.0, 0.0) * parts[-1][3]
    for at, v in enumerate((a, h, left)):
        yc_s[at, :blocks] = v
    yc_copies = spread("gy", dy, yc_s, yc_r)

    for copy in xc_copies:
        copy.wait_recv()
    x_global = global_coeffs(
        [tuple(xc_r[d, at * zc : (at + 1) * zc] for at in range(3)) for d in range(dx)]
    )
    for copy in xr_copies:
        copy.wait_recv()
    nodes = global_solve(
        [tuple(xr_r[d, at * zc : (at + 1) * zc] for at in range(2)) for d in range(dx)], x_global
    )
    for d in range(dx):
        xv_s[d, :zc] = nodes[d - 1] if d else jnp.zeros_like(nodes[0])
        xv_s[d, zc : 2 * zc] = nodes[d]
    xv_copies = spread("gx", dx, xv_s, xv_r)
    for copy in yc_copies:
        copy.wait_recv()
    y_global = global_coeffs(
        [tuple(yc_r[d, at, :blocks] for at in range(3)) for d in range(dy)]
    )
    for copy in xv_copies:
        copy.wait_recv()
    before = jnp.concatenate([xv_r[d, :zc] for d in range(dx)], axis=0)
    own = jnp.concatenate([xv_r[d, zc : 2 * zc] for d in range(dx)], axis=0)
    ends = expand(own, before, x_kept, x_scaled)
    v = jnp.concatenate(ends, axis=0)
    before = jnp.concatenate([before] + ends[:-1], axis=0)
    for j in range(mx - 1, -1, -1):
        if j < mx - 1:
            v = sx[j] + px[j] * before + wx[j] * v
        for k in range(X_CHUNKS):
            fs[pl.ds(k * mx + j, nz, stride=nx), :] = v[k * nz : (k + 1) * nz]

    for b in range(blocks):
        ts[pl.ds(b * LANES, LANES), :] = fs[pl.ds(b * LANES, LANES), :].T
    r = load_y(ts, 0, LANES, 0)
    left = jnp.zeros_like(r)
    for j in range(my - 1):
        left = left + r * py[j]
        sy[j] = r * qy[j]
        r = load_y(ts, j + 1, LANES, 0) + r * wy[j]
    (r, left), y_scaled = combine_sources(y_parts((r, left)), y_kept)
    yr_s[0, :blocks] = r
    yr_s[1, :blocks] = left
    yr_copies = spread("gy", dy, yr_s, yr_r)
    for copy in yr_copies:
        copy.wait_recv()
    nodes = global_solve(
        [tuple(yr_r[d, at, :blocks] for at in range(2)) for d in range(dy)], y_global
    )
    vnodes[0, :blocks] = jnp.zeros_like(nodes[0])
    for d in range(dy):
        vnodes[d + 1, :blocks] = nodes[d]
    before = vnodes[iy, :blocks]
    own = vnodes[iy + 1, :blocks]
    ends = expand(own, before, y_kept, y_scaled)
    for s in range(SUBS):
        vo[pl.ds(s, blocks, stride=SUBS), :] = ends[s]
        vp[pl.ds(s, blocks, stride=SUBS), :] = ends[s - 1] if s else before
    v = vo[...]
    before = vp[...]
    for j in range(my - 1, -1, -1):
        if j < my - 1:
            v = sy[j] + py[j] * before + wy[j] * v
        store_y(tv, j, v)
    for b in range(blocks):
        fs[pl.ds(b * LANES, LANES), :] = tv[pl.ds(b * LANES, LANES), :].T

    r = plane(fs, 0)
    for z in range(nz):
        fs[pl.ds(z * nx, nx), :] = r * plane(qz, z)
        if z + 1 < nz:
            r = plane(fs, z + 1) + r * plane(wz, z)
    v = None
    for z in range(nz - 1, -1, -1):
        v = plane(fs, z) if v is None else plane(fs, z) + plane(wz, z) * v
        out_ref[pl.ds(z * nx, nx), :] = plane(f_ref, z) + v

    for sent, copy in (
        (ix < dx - 1, x_up), (ix > 0, x_down), (iy < dy - 1, y_up), (iy > 0, y_down)
    ):
        pl.when(sent)(copy.wait_send)
    for copies in (xc_copies, xr_copies, xv_copies, yc_copies, yr_copies):
        for copy in copies:
            copy.wait_send()


def on_device(dx, dy, field, conductivity):
    nz, nx, ny = field.shape
    rows = nz * nx
    blocks = rows // LANES
    total_x = nx * dx
    total_y = ny * dy
    x_half = 0.5 * float(total_x * total_x // 16)
    y_half = 0.5 * float(total_y * total_y // 16)
    z_half = 0.5 * implicit_weight * depth_step
    zc = nz // dx
    span = LANES + 2 * PAD
    my = LANES // SUBS
    mx = nx // X_CHUNKS
    xrows = X_CHUNKS * nz
    yrows = blocks * SUBS
    b16 = ceil8(blocks)
    nsem = 4 + 3 * (dx - 1) + 2 * (dy - 1)

    def vmem(*shape):
        return pltpu.VMEM(shape, F32)

    grid = vmem(rows, LANES)
    out = pl.pallas_call(
        functools.partial(kernel, (nz, nx, dx, dy, x_half, y_half, z_half)),
        out_shape=jax.ShapeDtypeStruct((rows, LANES), F32),
        in_specs=[pl.BlockSpec(memory_space=pl.ANY)] * 2,
        out_specs=pl.BlockSpec(memory_space=pltpu.VMEM),
        scratch_shapes=[
            grid, grid,
            vmem(blocks * span, LANES), vmem(blocks * span, LANES), grid, grid, grid, grid, grid,
            vmem(my + 1, yrows, LANES),
            vmem(my - 1, yrows, LANES), vmem(my - 1, yrows, LANES), vmem(my - 1, yrows, LANES),
            vmem(my - 1, yrows, LANES),
            vmem(4, yrows, LANES), vmem(yrows, LANES), vmem(yrows, LANES),
            vmem(dy + 1, b16, LANES),
            vmem(mx + 1, xrows, LANES),
            vmem(mx - 1, xrows, LANES), vmem(mx - 1, xrows, LANES), vmem(mx - 1, xrows, LANES),
            vmem(mx - 1, xrows, LANES),
            grid, grid,
            vmem(2, 2, nz, LANES), vmem(2, 2, nz, LANES),
            vmem(2, 2, b16, LANES), vmem(2, 2, b16, LANES),
            vmem(dx, ceil8(3 * zc), LANES), vmem(dx, ceil8(3 * zc), LANES),
            vmem(dx, ceil8(2 * zc), LANES), vmem(dx, ceil8(2 * zc), LANES),
            vmem(dx, ceil8(2 * zc), LANES), vmem(dx, ceil8(2 * zc), LANES),
            vmem(3, b16, LANES), vmem(dy, 3, b16, LANES),
            vmem(2, b16, LANES), vmem(dy, 2, b16, LANES),
            pltpu.SemaphoreType.DMA((nsem,)), pltpu.SemaphoreType.DMA((nsem,)),
            pltpu.SemaphoreType.DMA((2 * LOADS,)),
        ],
        compiler_params=pltpu.CompilerParams(
            collective_id=0, has_side_effects=True, vmem_limit_bytes=54016 << 10
        ),
    )(field.reshape(rows, ny), conductivity.reshape(rows, ny))
    return out.reshape(nz, nx, ny)


def solution(mesh):
    return jax.shard_map(
        functools.partial(on_device, mesh.shape["gx"], mesh.shape["gy"]),
        mesh=mesh,
        in_specs=(P(None, "gx", "gy"), P(None, "gx", "gy")),
        out_specs=P(None, "gx", "gy"),
        check_vma=False,
    )
```

```python
import functools

import jax
import jax.numpy as jnp
from jax import lax
from jax.experimental import pallas as pl
from jax.experimental.pallas import tpu as pltpu
from jax.sharding import PartitionSpec as P

MESH = pl.DeviceIdType.MESH
F32 = jnp.float32
depth_step = 8.0
implicit_weight = 0.5

LANES = 128
SUBS = 8
PAD = SUBS
X_CHUNKS = 4
LOADS = 4


def ceil8(rows):
    return (rows + 7) // 8 * 8


def eliminate_cell(state, g):
    a, h, ground_left = state
    q = 1.0 / (a + h + g)
    w = g * q
    p = h * q
    return (a * w, h * w, ground_left + a * p), (w, p, q)


def combine_coeffs(parts):
    count = len(parts)

    def ground(k):
        return parts[k][0] + parts[k + 1][2] if k + 1 < count else parts[k][0]

    a, h, left = ground(0), parts[0][1], parts[0][2]
    kept = []
    for k in range(count - 1):
        (passed, h, left), factors = eliminate_cell((a, h, left), parts[k + 1][1])
        a = ground(k + 1) + passed
        kept.append(factors)
    return (a, h, left), kept


def combine_sources(parts, kept):
    count = len(parts)

    def source(k):
        return parts[k][0] + parts[k + 1][1] if k + 1 < count else parts[k][0]

    r, left = source(0), parts[0][1]
    scaled = []
    for k in range(count - 1):
        w, p, q = kept[k]
        left = left + r * p
        scaled.append(r * q)
        r = source(k + 1) + r * w
    return (r, left), scaled


def expand(own, before, kept, scaled):
    values = [own]
    for k in range(len(kept) - 1, -1, -1):
        w, p, _ = kept[k]
        values.append(scaled[k] + p * before + w * values[-1])
    return values[::-1]


def global_coeffs(parts):
    count = len(parts)

    def ground(d):
        return parts[d][0] + parts[d + 1][2] if d + 1 < count else parts[d][0]

    e = ground(0) + parts[0][1]
    kept = []
    for d in range(count - 1):
        g = parts[d + 1][1]
        q = 1.0 / (e + g)
        w = g * q
        kept.append((w, q))
        e = ground(d + 1) + e * w
    kept.append((None, 1.0 / e))
    return kept


def global_solve(parts, kept):
    count = len(parts)

    def source(d):
        return parts[d][0] + parts[d + 1][1] if d + 1 < count else parts[d][0]

    r = source(0)
    scaled = []
    for d in range(count - 1):
        w, q = kept[d]
        scaled.append(r * q)
        r = source(d + 1) + r * w
    values = [r * kept[-1][1]]
    for d in range(count - 2, -1, -1):
        values.append(scaled[d] + kept[d][0] * values[-1])
    return values[::-1]


def kernel(
    sizes, f_hbm, c_hbm, out_ref,
    f_ref, c_ref,
    tf, tc, te, ts, tv, ex, fs,
    gyc, wy, py, qy, sy, scr, vo, vp, vnodes,
    gx_, wx, px, qx, sx, wz, qz,
    xs, xr, ys, yr, xc_s, xc_r, xr_s, xr_r, xv_s, xv_r, yc_s, yc_r, yr_s, yr_r,
    ssem, rsem, lsem,
):
    nz, nx, dx, dy, x_half, y_half, z_half = sizes
    rows = nz * nx
    blocks = rows // LANES
    span = LANES + 2 * PAD
    my = LANES // SUBS
    mx = nx // X_CHUNKS
    zc = nz // dx
    ix = lax.axis_index("gx")
    iy = lax.axis_index("gy")

    barrier = pltpu.get_barrier_semaphore()
    for k in range(1, dx):
        pl.semaphore_signal(
            barrier, inc=1, device_id={"gx": lax.rem(ix + k, dx)}, device_id_type=MESH
        )
    for k in range(1, dy):
        pl.semaphore_signal(
            barrier, inc=1, device_id={"gy": lax.rem(iy + k, dy)}, device_id_type=MESH
        )

    loads = []
    piece = blocks // LOADS * LANES
    for k in range(LOADS):
        for at, (src, dst) in enumerate(((c_hbm, c_ref), (f_hbm, f_ref))):
            part = pl.ds(k * piece, piece)
            loads.append(pltpu.make_async_copy(src.at[part], dst.at[part], lsem.at[2 * k + at]))
            loads[-1].start()

    def remote(src, dst, at, target):
        return pltpu.make_async_remote_copy(
            src_ref=src, dst_ref=dst, send_sem=ssem.at[at], recv_sem=rsem.at[at],
            device_id=target, device_id_type=MESH,
        )

    for b in range(blocks):
        if b % (blocks // LOADS) == 0:
            at = 2 * (b // (blocks // LOADS))
            loads[at].wait()
            loads[at + 1].wait()
        tf[pl.ds(b * span + PAD, LANES), :] = f_ref[pl.ds(b * LANES, LANES), :].T
        tc[pl.ds(b * span + PAD, LANES), :] = c_ref[pl.ds(b * LANES, LANES), :].T
    for side, place in ((0, nx - 1), (1, 0)):
        xs[side, 0] = f_ref[pl.ds(place, nz, stride=nx), :]
        xs[side, 1] = c_ref[pl.ds(place, nz, stride=nx), :]
    for side, place in ((0, LANES - 1), (1, 0)):
        ys[side, 0, :blocks] = tf[pl.ds(PAD + place, blocks, stride=span), :]
        ys[side, 1, :blocks] = tc[pl.ds(PAD + place, blocks, stride=span), :]

    def load_y(ref, j, height, offset):
        return jnp.concatenate(
            [ref[pl.ds(b * height + offset + j, SUBS, stride=my), :] for b in range(blocks)],
            axis=0,
        )

    def store_y(ref, j, values):
        for b in range(blocks):
            ref[pl.ds(b * LANES + j, SUBS, stride=my), :] = values[b * SUBS : (b + 1) * SUBS]

    c_here, f_here = load_y(tc, 0, span, PAD), load_y(tf, 0, span, PAD)
    y_first = y_last = None
    for j in range(my - 1):
        c_next, f_next = load_y(tc, j + 1, span, PAD), load_y(tf, j + 1, span, PAD)
        g = y_half * (c_here + c_next)
        gyc[j + 1] = g
        new_flux = g * (f_next - f_here)
        if j == 0:
            y_first = new_flux
        else:
            store_y(te, j, 2.0 * (new_flux - y_last))
        c_here, f_here, y_last = c_next, f_next, new_flux

    def plane(ref, z):
        return ref[pl.ds(z * nx, nx), :]

    c_here, f_here = plane(c_ref, 0), plane(f_ref, 0)
    g = z_half * c_here
    excess = 1.0 + g
    flux = g * f_here
    for z in range(nz):
        if z + 1 < nz:
            c_next, f_next = plane(c_ref, z + 1), plane(f_ref, z + 1)
            g = z_half * (c_here + c_next)
            new_flux = g * (f_next - f_here)
        else:
            c_next, f_next = None, None
            g = z_half * c_here
            new_flux = -g * f_here
        q = 1.0 / (excess + g)
        w = g * q
        qz[pl.ds(z * nx, nx), :] = q
        wz[pl.ds(z * nx, nx), :] = w
        ex[pl.ds(z * nx, nx), :] = 2.0 * (new_flux - flux)
        excess = 1.0 + excess * w
        c_here, f_here, flux = c_next, f_next, new_flux

    pl.semaphore_wait(barrier, dx + dy - 2)

    x_up = remote(xs.at[0], xr.at[0], 0, {"gx": jnp.minimum(ix + 1, dx - 1)})
    x_down = remote(xs.at[1], xr.at[1], 1, {"gx": jnp.maximum(ix - 1, 0)})
    y_up = remote(ys.at[0], yr.at[0], 2, {"gy": jnp.minimum(iy + 1, dy - 1)})
    y_down = remote(ys.at[1], yr.at[1], 3, {"gy": jnp.maximum(iy - 1, 0)})
    for inside, copy in (
        (ix < dx - 1, x_up), (ix > 0, x_down), (iy < dy - 1, y_up), (iy > 0, y_down)
    ):
        pl.when(inside)(copy.start)

    def x_halo(side, inside, copy):
        pl.when(inside)(copy.wait_recv)

        @pl.when(jnp.logical_not(inside))
        def _():
            xr[side] = jnp.zeros(xr.shape[1:], F32)

    x_halo(0, ix > 0, x_up)
    x_halo(1, ix < dx - 1, x_down)

    def load_x(ref, which, j):
        pieces = []
        for k in range(X_CHUNKS):
            place = k * mx + j
            if place < 0:
                pieces.append(xr[0, which])
            elif place >= nx:
                pieces.append(xr[1, which])
            else:
                pieces.append(ref[pl.ds(place, nz, stride=nx), :])
        return jnp.concatenate(pieces, axis=0)

    c_here = load_x(c_ref, 1, 0)
    g = x_half * (load_x(c_ref, 1, -1) + c_here)
    gx_[0] = g
    state = (jnp.ones_like(g), g, jnp.zeros_like(g))
    for j in range(mx):
        c_next = load_x(c_ref, 1, j + 1)
        g = x_half * (c_here + c_next)
        gx_[j + 1] = g
        if j < mx - 1:
            (passed, h, left), (w, p, q) = eliminate_cell(state, g)
            wx[j], px[j], qx[j] = w, p, q
            state = (1.0 + passed, h, left)
        c_here = c_next

    def x_parts(arrays):
        return [tuple(v[k * nz : (k + 1) * nz] for v in arrays) for k in range(X_CHUNKS)]

    (a, h, left), x_kept = combine_coeffs(x_parts(state))
    a = a + jnp.where(ix == dx - 1, 1.0, 0.0) * g[(X_CHUNKS - 1) * nz :]
    for d in range(dx):
        for at, v in enumerate((a, h, left)):
            xc_s[d, at * zc : (at + 1) * zc] = v[d * zc : (d + 1) * zc]

    sems = [4]

    def spread(axis, count, src, dst):
        me = lax.axis_index(axis)
        copies = []
        for k in range(1, count):
            peer = lax.rem(me + k, count)
            piece = src.at[peer] if axis == "gx" else src
            copies.append(remote(piece, dst.at[me], sems[0], {axis: peer}))
            copies[-1].start()
            sems[0] += 1
        dst[me] = src[me] if axis == "gx" else src[...]
        return copies

    xc_copies = spread("gx", dx, xc_s, xc_r)

    def y_halo(side, inside, copy, place):
        pl.when(inside)(copy.wait_recv)

        @pl.when(jnp.logical_not(inside))
        def _():
            yr[side] = jnp.zeros(yr.shape[1:], F32)

        tf[pl.ds(place, blocks, stride=span), :] = yr[side, 0, :blocks]
        tc[pl.ds(place, blocks, stride=span), :] = yr[side, 1, :blocks]

    y_halo(0, iy > 0, y_up, PAD - 1)
    y_halo(1, iy < dy - 1, y_down, PAD + LANES)

    c_here, f_here = load_y(tc, 0, span, PAD), load_y(tf, 0, span, PAD)
    g = y_half * (load_y(tc, -1, span, PAD) + c_here)
    gyc[0] = g
    store_y(te, 0, 2.0 * (y_first - g * (f_here - load_y(tf, -1, span, PAD))))
    c_here, f_here = load_y(tc, my - 1, span, PAD), load_y(tf, my - 1, span, PAD)
    g = y_half * (c_here + load_y(tc, my, span, PAD))
    gyc[my] = g
    store_y(te, my - 1, 2.0 * (g * (load_y(tf, my, span, PAD) - f_here) - y_last))
    for b in range(blocks):
        ex[pl.ds(b * LANES, LANES), :] += te[pl.ds(b * LANES, LANES), :].T

    f_here = load_x(f_ref, 0, 0)
    flux = gx_[0] * (f_here - load_x(f_ref, 0, -1))
    r = None
    for j in range(mx):
        f_next = load_x(f_ref, 0, j + 1)
        new_flux = gx_[j + 1] * (f_next - f_here)
        source = 2.0 * (new_flux - flux) + load_x(ex, None, j)
        if r is None:
            r, left = source, jnp.zeros_like(source)
        else:
            left = left + r * px[j - 1]
            sx[j - 1] = r * qx[j - 1]
            r = source + r * wx[j - 1]
        f_here, flux = f_next, new_flux
    (r, left), x_scaled = combine_sources(x_parts((r, left)), x_kept)
    for d in range(dx):
        for at, v in enumerate((r, left)):
            xr_s[d, at * zc : (at + 1) * zc] = v[d * zc : (d + 1) * zc]
    xr_copies = spread("gx", dx, xr_s, xr_r)

    g = gyc[0]
    state = (jnp.ones_like(g), g, jnp.zeros_like(g))
    for j in range(my - 1):
        (passed, h, left), (w, p, q) = eliminate_cell(state, gyc[j + 1])
        wy[j], py[j], qy[j] = w, p, q
        state = (1.0 + passed, h, left)

    def y_parts(arrays):
        for at, v in enumerate(arrays):
            scr[at] = v
        return [
            tuple(scr[at, pl.ds(s, blocks, stride=SUBS), :] for at in range(len(arrays)))
            for s in range(SUBS)
        ]

    parts = y_parts((*state, gyc[my]))
    (a, h, left), y_kept = combine_coeffs([part[:3] for part in parts])
    a = a + jnp.where(iy == dy - 1, 1.0, 0.0) * parts[-1][3]
    for at, v in enumerate((a, h, left)):
        yc_s[at, :blocks] = v
    yc_copies = spread("gy", dy, yc_s, yc_r)

    for copy in xc_copies:
        copy.wait_recv()
    x_global = global_coeffs(
        [tuple(xc_r[d, at * zc : (at + 1) * zc] for at in range(3)) for d in range(dx)]
    )
    for copy in xr_copies:
        copy.wait_recv()
    nodes = global_solve(
        [tuple(xr_r[d, at * zc : (at + 1) * zc] for at in range(2)) for d in range(dx)], x_global
    )
    for d in range(dx):
        xv_s[d, :zc] = nodes[d - 1] if d else jnp.zeros_like(nodes[0])
        xv_s[d, zc : 2 * zc] = nodes[d]
    xv_copies = spread("gx", dx, xv_s, xv_r)
    for copy in yc_copies:
        copy.wait_recv()
    y_global = global_coeffs(
        [tuple(yc_r[d, at, :blocks] for at in range(3)) for d in range(dy)]
    )
    for copy in xv_copies:
        copy.wait_recv()
    before = jnp.concatenate([xv_r[d, :zc] for d in range(dx)], axis=0)
    own = jnp.concatenate([xv_r[d, zc : 2 * zc] for d in range(dx)], axis=0)
    ends = expand(own, before, x_kept, x_scaled)
    v = jnp.concatenate(ends, axis=0)
    before = jnp.concatenate([before] + ends[:-1], axis=0)
    for j in range(mx - 1, -1, -1):
        if j < mx - 1:
            v = sx[j] + px[j] * before + wx[j] * v
        for k in range(X_CHUNKS):
            fs[pl.ds(k * mx + j, nz, stride=nx), :] = v[k * nz : (k + 1) * nz]

    for b in range(blocks):
        ts[pl.ds(b * LANES, LANES), :] = fs[pl.ds(b * LANES, LANES), :].T
    r = load_y(ts, 0, LANES, 0)
    left = jnp.zeros_like(r)
    for j in range(my - 1):
        left = left + r * py[j]
        sy[j] = r * qy[j]
        r = load_y(ts, j + 1, LANES, 0) + r * wy[j]
    (r, left), y_scaled = combine_sources(y_parts((r, left)), y_kept)
    yr_s[0, :blocks] = r
    yr_s[1, :blocks] = left
    yr_copies = spread("gy", dy, yr_s, yr_r)
    for copy in yr_copies:
        copy.wait_recv()
    nodes = global_solve(
        [tuple(yr_r[d, at, :blocks] for at in range(2)) for d in range(dy)], y_global
    )
    vnodes[0, :blocks] = jnp.zeros_like(nodes[0])
    for d in range(dy):
        vnodes[d + 1, :blocks] = nodes[d]
    before = vnodes[iy, :blocks]
    own = vnodes[iy + 1, :blocks]
    ends = expand(own, before, y_kept, y_scaled)
    for s in range(SUBS):
        vo[pl.ds(s, blocks, stride=SUBS), :] = ends[s]
        vp[pl.ds(s, blocks, stride=SUBS), :] = ends[s - 1] if s else before
    v = vo[...]
    before = vp[...]
    for j in range(my - 1, -1, -1):
        if j < my - 1:
            v = sy[j] + py[j] * before + wy[j] * v
        store_y(tv, j, v)
    for b in range(blocks):
        fs[pl.ds(b * LANES, LANES), :] = tv[pl.ds(b * LANES, LANES), :].T

    r = plane(fs, 0)
    for z in range(nz):
        fs[pl.ds(z * nx, nx), :] = r * plane(qz, z)
        if z + 1 < nz:
            r = plane(fs, z + 1) + r * plane(wz, z)
    v = None
    for z in range(nz - 1, -1, -1):
        v = plane(fs, z) if v is None else plane(fs, z) + plane(wz, z) * v
        out_ref[pl.ds(z * nx, nx), :] = plane(f_ref, z) + v

    for sent, copy in (
        (ix < dx - 1, x_up), (ix > 0, x_down), (iy < dy - 1, y_up), (iy > 0, y_down)
    ):
        pl.when(sent)(copy.wait_send)
    for copies in (xc_copies, xr_copies, xv_copies, yc_copies, yr_copies):
        for copy in copies:
            copy.wait_send()


def on_device(dx, dy, field, conductivity):
    nz, nx, ny = field.shape
    rows = nz * nx
    blocks = rows // LANES
    total_x = nx * dx
    total_y = ny * dy
    x_half = 0.5 * float(total_x * total_x // 16)
    y_half = 0.5 * float(total_y * total_y // 16)
    z_half = 0.5 * implicit_weight * depth_step
    zc = nz // dx
    span = LANES + 2 * PAD
    my = LANES // SUBS
    mx = nx // X_CHUNKS
    xrows = X_CHUNKS * nz
    yrows = blocks * SUBS
    b16 = ceil8(blocks)
    nsem = 4 + 3 * (dx - 1) + 2 * (dy - 1)

    def vmem(*shape):
        return pltpu.VMEM(shape, F32)

    grid = vmem(rows, LANES)
    out = pl.pallas_call(
        functools.partial(kernel, (nz, nx, dx, dy, x_half, y_half, z_half)),
        out_shape=jax.ShapeDtypeStruct((rows, LANES), F32),
        in_specs=[pl.BlockSpec(memory_space=pl.ANY)] * 2,
        out_specs=pl.BlockSpec(memory_space=pltpu.VMEM),
        scratch_shapes=[
            grid, grid,
            vmem(blocks * span, LANES), vmem(blocks * span, LANES), grid, grid, grid, grid, grid,
            vmem(my + 1, yrows, LANES),
            vmem(my - 1, yrows, LANES), vmem(my - 1, yrows, LANES), vmem(my - 1, yrows, LANES),
            vmem(my - 1, yrows, LANES),
            vmem(4, yrows, LANES), vmem(yrows, LANES), vmem(yrows, LANES),
            vmem(dy + 1, b16, LANES),
            vmem(mx + 1, xrows, LANES),
            vmem(mx - 1, xrows, LANES), vmem(mx - 1, xrows, LANES), vmem(mx - 1, xrows, LANES),
            vmem(mx - 1, xrows, LANES),
            grid, grid,
            vmem(2, 2, nz, LANES), vmem(2, 2, nz, LANES),
            vmem(2, 2, b16, LANES), vmem(2, 2, b16, LANES),
            vmem(dx, ceil8(3 * zc), LANES), vmem(dx, ceil8(3 * zc), LANES),
            vmem(dx, ceil8(2 * zc), LANES), vmem(dx, ceil8(2 * zc), LANES),
            vmem(dx, ceil8(2 * zc), LANES), vmem(dx, ceil8(2 * zc), LANES),
            vmem(3, b16, LANES), vmem(dy, 3, b16, LANES),
            vmem(2, b16, LANES), vmem(dy, 2, b16, LANES),
            pltpu.SemaphoreType.DMA((nsem,)), pltpu.SemaphoreType.DMA((nsem,)),
            pltpu.SemaphoreType.DMA((2 * LOADS,)),
        ],
        compiler_params=pltpu.CompilerParams(
            collective_id=0, has_side_effects=True, vmem_limit_bytes=54016 << 10
        ),
    )(field.reshape(rows, ny), conductivity.reshape(rows, ny))
    return out.reshape(nz, nx, ny)


def solution(mesh):
    return jax.shard_map(
        functools.partial(on_device, mesh.shape["gx"], mesh.shape["gy"]),
        mesh=mesh,
        in_specs=(P(None, "gx", "gy"), P(None, "gx", "gy")),
        out_specs=P(None, "gx", "gy"),
        check_vma=False,
    )
```
